32 devices in a mesh: groups: 2 (over x), depth: 16 (over z, y, core).
Axes of the slice: x: 2, y: 2, z: 4, core: 2. Of those that a mesh axis runs over, the one named last changes fastest.
Arguments:
- voxels: bfloat16 [256, 32, 16384], P(('groups', 'depth')), parts along dimension 0, may hold values from -6 to 6
- offsets: int32 [256], P('groups'), parts along dimension 0, may hold values from 0 to 127
- w_first: bfloat16 [64, 32], replicated, may hold values from -1 to 1
- decoder_second_weight: bfloat16 [33, 64], replicated, may hold values from -0.75 to 0.75
- cotangent: float32 [32, 32768], P(None, ('groups', 'depth')), parts along dimension 1, may hold values from -6 to 6
Outputs:
- image: float32 [32, 32768], P(None, ('groups', 'depth')), parts along dimension 1
- grad_voxels: bfloat16 [256, 32, 16384], P(('groups', 'depth')), parts along dimension 0
- grad_first: float32 [128, 32], P('groups'), parts along dimension 0
- grad_second: float32 [66, 64], P('groups'), parts along dimension 0
The draws below stay inside these ranges and needn't reach their ends.
There are 2 independent parts, one for each index of `groups`. The reference program is written for one: setup_inputs(seed, part) draws one part's arguments, and reference() takes and returns one part's arrays. A program takes and returns all parts, laid end to end along the dimension named above; an argument that names none is the same for every part. Nothing has to cross between parts.
Inputs may be any that keep to these rules, and one draw needn't show every extreme that they name: offsets[p] counts tiles of 128 rays.
All inputs are finite; a program needn't handle non-finite values.
Results may differ from the reference program's by a relative error of at most 0.0085.
Values may be sent and summed in bfloat16 or wider, within the bound.
A program may use at most 192 MiB of HBM per device.

```python
import jax
import jax.numpy as jnp
from jax import lax

F = 32
H = 64
C = 32
TILE = 128
RAYS = 16384
NPL = 128


def plant(result, own_key, smallest, top_value):
    extent = result.shape
    place = [jax.random.randint(jax.random.fold_in(own_key, axis), (), 0, extent[axis]) for axis in range(len(extent))]
    result = result.at[tuple(place)].set(smallest)
    longest = extent.index(max(extent))
    place[longest] = (place[longest] + 1) % extent[longest]
    return result.at[tuple(place)].set(top_value)


def shard_levels(rng, shape, shards, smallest, high):
    level, own = 1.0, jax.random.fold_in(rng, 6)
    for dim, shards_of in shards:
        heights = jnp.exp(jax.random.uniform(jax.random.fold_in(own, dim), (shards_of,), jnp.float32, smallest / len(shards), high / len(shards)))
        level = level * jnp.repeat(heights, shape[dim] // shards_of).reshape([-1 if axis == dim else 1 for axis in range(len(shape))])
    return level


def normal_values(own_key, extent, spread, limit, shards=(), dtype=jnp.bfloat16):
    result = spread * jax.random.normal(own_key, extent, jnp.float32)
    if shards:
        result = result * shard_levels(own_key, extent, shards, -0.22, 0.18)
    return jnp.clip(result, -limit, limit).astype(dtype)


def setup_inputs(seed: int = 0, part: int = 0) -> dict:
    key_of = jax.random.split(jax.random.key(seed), 6)
    part_splits = jax.random.split(jax.random.fold_in(key_of[5], part), 6)
    return {
        "voxels": normal_values(part_splits[0], (NPL, F, RAYS), 1.0, 6.0, ((0, 16),)),
        "offsets": plant(jax.random.randint(part_splits[1], (NPL,), 0, RAYS // TILE), jax.random.fold_in(part_splits[1], 1), 0, (RAYS // TILE) - 1).astype(jnp.int32),
        "w_first": normal_values(key_of[2], (H, F), F ** -0.5, 1.0),
        "decoder_second_weight": normal_values(key_of[3], (C + 1, H), H ** -0.5, 0.75),
        "cotangent": normal_values(part_splits[4], (C, RAYS), 1.0, 6.0, ((1, 16),), jnp.float32),
    }


def decode_plane(plane, w_first, decoder_second_weight):
    preact = jnp.dot(w_first, plane, preferred_element_type=jnp.float32)
    hidden = jax.nn.silu(preact).astype(jnp.bfloat16)
    output_raw = jnp.dot(decoder_second_weight, hidden, preferred_element_type=jnp.float32)
    return preact, hidden, output_raw


def make_slab(output_raw, dscale):
    channels = output_raw.shape[0] - 1
    emitted_light = jax.nn.sigmoid(output_raw[:channels])
    density = jax.nn.softplus(output_raw[channels]) * dscale
    return jnp.concatenate([emitted_light, density[None]], 0).astype(jnp.bfloat16)


def move_rays(values, start):
    doubled = jnp.concatenate([values, values], values.ndim - 1)
    return lax.dynamic_slice_in_dim(doubled, start.astype(jnp.int32), values.shape[-1], values.ndim - 1)


def blended_image(slabs, upstream_gradient):
    channels = slabs.shape[1] - 1
    emitted_light = slabs[:, :channels].astype(jnp.float32)
    density = slabs[:, channels].astype(jnp.float32)
    passing = jnp.exp(-density)
    through = jnp.cumprod(passing, axis=0)
    before = jnp.concatenate([jnp.ones_like(through[:1]), through[:-1]], 0)
    sample_weight_rows = before * (1.0 - passing)
    pixel_colour = jnp.einsum("vi,vsi->si", sample_weight_rows, emitted_light)
    objective_value = jnp.einsum("vz,dvz->dz", upstream_gradient, emitted_light)
    running = jnp.cumsum(sample_weight_rows * objective_value, axis=0)
    return passing, before, sample_weight_rows, objective_value, running, through[-1], pixel_colour


def slab_gradient(passing, before, sample_weight_rows, objective_value, running, upstream_gradient, enter, prior, ray_total):
    grad_rad = (enter * sample_weight_rows)[:, None, :] * upstream_gradient[None]
    grad_dens = enter * before * passing * objective_value - (ray_total - (prior + enter * running))
    return jnp.concatenate([grad_rad, grad_dens[:, None, :]], 1).astype(jnp.bfloat16)


def plane_backward(carry, inputs, w_first, decoder_second_weight, dscale):
    plane, grad_sheared, shift_tiles = inputs
    rays_count = plane.shape[1]
    preact, hidden, output_raw = decode_plane(plane, w_first, decoder_second_weight)
    grad_slab = move_rays(grad_sheared, rays_count - TILE * shift_tiles).astype(jnp.float32)
    channels = output_raw.shape[0] - 1
    sig_rad = jax.nn.sigmoid(output_raw[:channels])
    grad_rad = grad_slab[:channels] * sig_rad * (1.0 - sig_rad)
    grad_dens = grad_slab[channels] * dscale * jax.nn.sigmoid(output_raw[channels])
    grad_raw = jnp.concatenate([grad_rad, grad_dens[None]], 0).astype(jnp.bfloat16)
    grad_hidden = jnp.dot(decoder_second_weight.T, grad_raw, preferred_element_type=jnp.float32)
    sig_pre = jax.nn.sigmoid(preact)
    grad_pre = (grad_hidden * sig_pre * (1.0 + preact * (1.0 - sig_pre))).astype(jnp.bfloat16)
    grad_plane = jnp.dot(w_first.T, grad_pre, preferred_element_type=jnp.float32).astype(jnp.bfloat16)
    contract = (((1,), (1,)), ((), ()))
    acc_first = carry[0] + lax.dot_general(grad_pre, plane, contract, preferred_element_type=jnp.float32)
    acc_second = carry[1] + lax.dot_general(grad_raw, hidden, contract, preferred_element_type=jnp.float32)
    return (acc_first, acc_second), grad_plane


def reference(voxels, offsets, w_first, decoder_second_weight, cotangent):
    dscale = 3.0 / NPL

    def forward_plane(inputs):
        plane, shift_tiles = inputs
        output_raw = decode_plane(plane, w_first, decoder_second_weight)[2]
        return move_rays(make_slab(output_raw, dscale), TILE * shift_tiles)

    slabs = lax.map(forward_plane, (voxels, offsets))
    passing, before, sample_weight_rows, objective_value, running, last_pass, image = blended_image(slabs, cotangent)
    ray_total = jnp.sum(cotangent * image, axis=0)
    grad_sheared = slab_gradient(passing, before, sample_weight_rows, objective_value, running, cotangent, 1.0, 0.0, ray_total)

    def step_plane(carry, inputs):
        return plane_backward(carry, inputs, w_first, decoder_second_weight, dscale)

    start = (jnp.zeros(w_first.shape, jnp.float32), jnp.zeros(decoder_second_weight.shape, jnp.float32))
    grads, grad_voxels = lax.scan(step_plane, start, (voxels, grad_sheared, offsets))
    return image, grad_voxels, grads[0], grads[1]
```

```python
import functools

import jax
import jax.numpy as jnp
from jax import lax
from jax.experimental import pallas as pl
from jax.experimental.pallas import tpu as pltpu
from jax.sharding import PartitionSpec as P

TILE = 128
PACK = 4
BF = jnp.bfloat16
F32 = jnp.float32
NT = (((1,), (1,)), ((), ()))


def dot(a, b):
    return jnp.dot(a, b, preferred_element_type=F32)


def running_sum(x):
    rows = x.shape[0]
    row = lax.broadcasted_iota(jnp.int32, x.shape, 0)
    s = 1
    while s < rows:
        x = x + jnp.where(row >= s, pltpu.roll(x, s, 0), 0.0)
        s *= 2
    return x


def gather_tiles(off_ref, vox_ref, x_ref, step):
    planes, feats, rays = vox_ref.shape
    tiles = x_ref.shape[1] // TILE
    total = rays // TILE
    for p in range(planes):
        for j in range(tiles):
            t = lax.rem(step * tiles + j + off_ref[p], total)
            x_ref[pl.ds(p * feats, feats), pl.ds(j * TILE, TILE)] = vox_ref[
                p, :, pl.ds(pl.multiple_of(t * TILE, TILE), TILE)
            ]


def absorb(dens):
    upto = running_sum(dens)
    passing = jnp.exp(-dens)
    before = jnp.exp(dens - upto)
    return upto, passing, before


def softplus(x):
    return jnp.maximum(x, 0.0) + jnp.log1p(jnp.exp(-jnp.abs(x)))


def forward_kernel(dscale, off_ref, vox_ref, w1_ref, w2_ref, col_ref, last_ref, x_ref, rad_ref):
    step = pl.program_id(0)
    gather_tiles(off_ref, vox_ref, x_ref, step)
    halves, rows = w2_ref.shape[0], w2_ref.shape[1]
    planes = vox_ref.shape[0]
    wide = rows - planes
    kin = w1_ref.shape[1]
    raw_d = None
    for h in range(halves):
        half = dot(w1_ref[...], x_ref[pl.ds(h * kin, kin), :])
        hidden = (half + half * jnp.tanh(half)).astype(BF)
        raw = dot(w2_ref[h], hidden)
        rad_ref[pl.ds(h * wide, wide), :] = 0.5 * jnp.tanh(raw[:wide]) + 0.5
        d = raw[wide:]
        raw_d = d if raw_d is None else raw_d + d
    dens = softplus(raw_d) * dscale
    upto, passing, before = absorb(dens)
    weight = before * (1.0 - passing)
    chans = col_ref.shape[1]
    colour = None
    for p in range(planes):
        term = weight[p : p + 1] * rad_ref[pl.ds(p * chans, chans), :]
        colour = term if colour is None else colour + term
    col_ref[0] = colour
    last_ref[0] = jnp.exp(-upto[planes - 1 : planes])


def backward_kernel(
    dscale,
    off_ref,
    vox_ref,
    w1_ref,
    w2_ref,
    w1t_ref,
    w2t_ref,
    ones_ref,
    cot_ref,
    state_ref,
    gvox_ref,
    acc1_ref,
    acc2_ref,
    x_ref,
    half_ref,
    tanh_ref,
    hid_ref,
    slope_ref,
    graw_ref,
    prod_ref,
):
    step = pl.program_id(0)

    @pl.when(step == 0)
    def _():
        acc1_ref[...] = jnp.zeros_like(acc1_ref)
        acc2_ref[...] = jnp.zeros_like(acc2_ref)

    gather_tiles(off_ref, vox_ref, x_ref, step)
    halves, rows = w2_ref.shape[0], w2_ref.shape[1]
    planes, feats, rays = vox_ref.shape
    wide = rows - planes
    kin = w1_ref.shape[1]
    kmid = w1_ref.shape[0]
    chans = cot_ref.shape[1]
    cot = cot_ref[0].astype(F32)
    raw_d = None
    for h in range(halves):
        half = dot(w1_ref[...], x_ref[pl.ds(h * kin, kin), :])
        t = jnp.tanh(half)
        half_ref[pl.ds(h * kmid, kmid), :] = (1.0 + t) * (1.0 + half * (1.0 - t))
        hidden = (half + half * t).astype(BF)
        hid_ref[pl.ds(h * kmid, kmid), :] = hidden
        raw = dot(w2_ref[h], hidden)
        s = jnp.tanh(raw[:wide])
        slope_ref[pl.ds(h * wide, wide), :] = 0.25 - 0.25 * s * s
        for k in range(PACK):
            prod_ref[pl.ds(h * wide + k * chans, chans), :] = (
                cot * (0.5 * s[k * chans : (k + 1) * chans] + 0.5)
            ).astype(BF)
        d = raw[wide:]
        raw_d = d if raw_d is None else raw_d + d
    score = dot(ones_ref[...], prod_ref[...])
    dens = softplus(raw_d) * dscale
    upto, passing, before = absorb(dens)
    enter = state_ref[0, 0:1, :]
    rest = state_ref[0, 1:2, :]
    before = enter * before
    weight = before * (1.0 - passing)
    running = running_sum(weight * score)
    grad_d = before * passing * score - (rest - running)
    grad_d = (grad_d * (dscale * (0.5 * jnp.tanh(0.5 * raw_d) + 0.5))).astype(BF)
    for h in range(halves):
        for k in range(PACK):
            p = h * PACK + k
            graw_ref[h, pl.ds(k * chans, chans), :] = (
                (weight[p : p + 1] * cot) * slope_ref[pl.ds(p * chans, chans), :]
            ).astype(BF)
        graw_ref[h, pl.ds(wide, planes), :] = grad_d
        graw = graw_ref[h]
        ghid = dot(w2t_ref[h], graw)
        gpre = (ghid * half_ref[pl.ds(h * kmid, kmid), :]).astype(BF)
        gx = dot(w1t_ref[...], gpre).astype(BF)
        x = x_ref[pl.ds(h * kin, kin), :]
        acc1_ref[...] += lax.dot_general(gpre, x, NT, preferred_element_type=F32)
        acc2_ref[h] += lax.dot_general(
            graw, hid_ref[pl.ds(h * kmid, kmid), :], NT, preferred_element_type=F32
        )
        tiles = x_ref.shape[1] // TILE
        for k in range(PACK):
            p = h * PACK + k
            for j in range(tiles):
                t = lax.rem(step * tiles + j + off_ref[p], rays // TILE)
                gvox_ref[p, :, pl.ds(pl.multiple_of(t * TILE, TILE), TILE)] = gx[
                    k * feats : (k + 1) * feats, j * TILE : (j + 1) * TILE
                ]


def greet(n, me):
    barrier = pltpu.get_barrier_semaphore()
    for s in range(1, n):
        pl.semaphore_signal(
            barrier,
            inc=1,
            device_id={"depth": lax.rem(me + s, n)},
            device_id_type=pl.DeviceIdType.MESH,
        )
    pl.semaphore_wait(barrier, n - 1)


def swap(n, me, source, target, send_sem, recv_sem):
    copies = []
    for s in range(1, n):
        to = lax.rem(me + s, n)
        copies.append(
            pltpu.make_async_remote_copy(
                src_ref=source(to),
                dst_ref=target.at[me],
                send_sem=send_sem.at[s],
                recv_sem=recv_sem.at[s],
                device_id={"depth": to},
                device_id_type=pl.DeviceIdType.MESH,
            )
        )
    for copy in copies:
        copy.start()
    return copies


def state_kernel(n, last_ref, col_ref, cot_ref, out_ref, mine, got, back, s1, r1, s2, r2):
    me = lax.axis_index("depth")
    greet(n, me)

    def fill(d, carry):
        mine[d, 0:1, :] = last_ref[d]
        mine[d, 1:2, :] = jnp.sum(col_ref[d] * cot_ref[d].astype(F32), axis=0, keepdims=True)
        return carry

    lax.fori_loop(0, n, fill, 0)
    copies = swap(n, me, lambda to: mine.at[to], got, s1, r1)
    got[me] = mine[me]
    for copy in copies:
        copy.wait()
    enter = jnp.ones_like(got[0, 0:1, :])
    prior = jnp.zeros_like(enter)
    for d in range(n):
        back[d, 0:1, :] = enter
        back[d, 1:2, :] = prior
        prior = prior + enter * got[d, 1:2, :]
        enter = enter * got[d, 0:1, :]
    for d in range(n):
        back[d, 1:2, :] = prior - back[d, 1:2, :]
    copies = swap(n, me, lambda to: back.at[to], out_ref, s2, r2)
    out_ref[me] = back[me]
    for copy in copies:
        copy.wait()


def exchange_state(n, last, colour, cot):
    chunk = last.shape[2]
    shape = (n, 2, chunk)
    vmem = pl.BlockSpec(memory_space=pltpu.VMEM)
    return pl.pallas_call(
        functools.partial(state_kernel, n),
        out_shape=jax.ShapeDtypeStruct(shape, F32),
        in_specs=[vmem] * 3,
        out_specs=vmem,
        scratch_shapes=[pltpu.VMEM(shape, F32)] * 3 + [pltpu.SemaphoreType.DMA((n,))] * 4,
        compiler_params=pltpu.CompilerParams(collective_id=1, has_side_effects=True),
        name="exchange_state",
    )(last, colour, cot)


def total_kernel(n, in_ref, out_ref, got, mine, s1, r1, s2, r2):
    me = lax.axis_index("depth")
    greet(n, me)
    copies = swap(n, me, lambda to: in_ref.at[to], got, s1, r1)
    got[me] = in_ref[me]
    for copy in copies:
        copy.wait()
    mine[...] = jnp.sum(got[...], axis=0)
    copies = swap(n, me, lambda to: mine, out_ref, s2, r2)
    out_ref[me] = mine[...]
    for copy in copies:
        copy.wait()


def total_over_depth(n, x):
    vmem = pl.BlockSpec(memory_space=pltpu.VMEM)
    return pl.pallas_call(
        functools.partial(total_kernel, n),
        out_shape=jax.ShapeDtypeStruct(x.shape, F32),
        in_specs=[vmem],
        out_specs=vmem,
        scratch_shapes=[pltpu.VMEM(x.shape, F32), pltpu.VMEM(x.shape[1:], F32)]
        + [pltpu.SemaphoreType.DMA((n,))] * 4,
        compiler_params=pltpu.CompilerParams(collective_id=2, has_side_effects=True),
        name="total_over_depth",
    )(x)


def block_weights(w_first, w_second, planes):
    halves = planes // PACK
    eye = jnp.eye(PACK, dtype=BF)
    w1 = jnp.kron(eye, w_first)
    rad = jnp.kron(eye, w_second[:-1])
    spot = jnp.eye(planes, dtype=BF).reshape(planes, halves, PACK)
    dens = jnp.einsum("phk,j->hpkj", spot, w_second[-1]).reshape(halves, planes, -1)
    rad = jnp.broadcast_to(rad, (halves,) + rad.shape)
    half = jnp.asarray(0.5, BF)
    w2 = jnp.concatenate([rad * half, dens], 1)
    w2t = jnp.concatenate([rad, dens], 1).swapaxes(1, 2) * half
    return w1 * half, w2, w1.T, w2t


def shards(voxels, offsets, w_first, w_second, cotangent):
    planes, feats, rays = voxels.shape
    hid = w_first.shape[0]
    chans, chunk = cotangent.shape
    n = lax.axis_size("depth")
    halves = planes // PACK
    dscale = 3.0 / (planes * n)
    block = min(512, chunk)
    per = chunk // block
    steps = rays // block
    my_off = lax.dynamic_slice_in_dim(offsets, lax.axis_index("depth") * planes, planes)
    w1, w2, w1t, w2t = block_weights(w_first, w_second, planes)
    cot = lax.all_gather(cotangent.astype(BF), "depth")

    smem = pl.BlockSpec(memory_space=pltpu.SMEM)
    vmem = pl.BlockSpec(memory_space=pltpu.VMEM)

    def ray_spec(rows):
        return pl.BlockSpec((1, rows, block), lambda i: (i // per, 0, i % per))

    params = pltpu.CompilerParams(vmem_limit_bytes=60 * 2**20)
    colour, last = pl.pallas_call(
        functools.partial(forward_kernel, dscale),
        grid=(steps,),
        out_shape=(
            jax.ShapeDtypeStruct((n, chans, chunk), F32),
            jax.ShapeDtypeStruct((n, 1, chunk), F32),
        ),
        in_specs=[smem] + [vmem] * 3,
        out_specs=(ray_spec(chans), ray_spec(1)),
        scratch_shapes=[
            pltpu.VMEM((planes * feats, block), BF),
            pltpu.VMEM((planes * chans, block), F32),
        ],
        compiler_params=params,
        cost_estimate=pl.CostEstimate(
            flops=8 * 10**9, bytes_accessed=12 * 2**20, transcendentals=10**7
        ),
        name="forward",
    )(my_off, voxels, w1, w2)
    state = exchange_state(n, last, colour, cot)
    share = (state[:, 0:1, :] * colour).astype(BF)
    image = lax.psum_scatter(share, "depth", scatter_dimension=0).astype(F32)
    ones = jnp.kron(jnp.eye(planes, dtype=BF), jnp.ones((1, chans), BF))
    rows = PACK * chans + planes
    gvox, acc1, acc2 = pl.pallas_call(
        functools.partial(backward_kernel, dscale),
        grid=(steps,),
        out_shape=(
            jax.ShapeDtypeStruct(voxels.shape, BF),
            jax.ShapeDtypeStruct((PACK * hid, PACK * feats), F32),
            jax.ShapeDtypeStruct((halves, rows, PACK * hid), F32),
        ),
        in_specs=[smem] + [vmem] * 6 + [ray_spec(chans), ray_spec(2)],
        out_specs=(vmem, vmem, vmem),
        scratch_shapes=[
            pltpu.VMEM((planes * feats, block), BF),
            pltpu.VMEM((planes * hid, block), F32),
            pltpu.VMEM((8, 128), F32),
            pltpu.VMEM((planes * hid, block), BF),
            pltpu.VMEM((planes * chans, block), F32),
            pltpu.VMEM((halves, rows, block), BF),
            pltpu.VMEM((planes * chans, block), BF),
        ],
        compiler_params=params,
        cost_estimate=pl.CostEstimate(
            flops=60 * 10**9, bytes_accessed=24 * 2**20, transcendentals=10**7
        ),
        name="backward",
    )(my_off, voxels, w1, w2, w1t, w2t, ones, cot, state)
    g1 = sum(
        acc1[k * hid : (k + 1) * hid, k * feats : (k + 1) * feats] for k in range(PACK)
    )
    g2 = jnp.zeros((chans, hid), F32)
    gd = jnp.zeros((1, hid), F32)
    for h in range(halves):
        for k in range(PACK):
            cols = slice(k * hid, (k + 1) * hid)
            row = PACK * chans + h * PACK + k
            g2 = g2 + acc2[h, k * chans : (k + 1) * chans, cols]
            gd = gd + acc2[h, row : row + 1, cols]
    flat = jnp.concatenate([g1.reshape(-1), g2.reshape(-1), gd.reshape(-1)])
    piece = -(-flat.size // (n * 128)) * 128
    padded = jnp.pad(flat, (0, n * piece - flat.size)).reshape(n, 1, piece)
    summed = total_over_depth(n, padded).reshape(-1)
    cut = g1.size
    grad_first = summed[:cut].reshape(g1.shape)
    grad_second = summed[cut : flat.size].reshape(chans + 1, hid)
    return image, gvox, grad_first, grad_second


def solution(mesh):
    placed = (
        P(("groups", "depth"), None, None),
        P("groups"),
        P(),
        P(),
        P(None, ("groups", "depth")),
    )
    return jax.shard_map(
        shards,
        mesh=mesh,
        in_specs=placed,
        out_specs=(
            P(None, ("groups", "depth")),
            P(("groups", "depth"), None, None),
            P("groups", None),
            P("groups", None),
        ),
        check_vma=False,
    )
```

```python
import functools

import jax
import jax.numpy as jnp
from jax import lax
from jax.experimental import pallas as pl
from jax.experimental.pallas import tpu as pltpu
from jax.sharding import PartitionSpec as P

TILE = 128
PACK = 4
BLOCK = 1024
FSUB = 1024
BSUB = 1024
BF = jnp.bfloat16
F32 = jnp.float32
NT = (((1,), (1,)), ((), ()))


def dot(a, b):
    return jnp.dot(a, b, preferred_element_type=F32)


def running_sum(x):
    rows = x.shape[0]
    row = lax.broadcasted_iota(jnp.int32, x.shape, 0)
    s = 1
    while s < rows:
        x = x + jnp.where(row >= s, pltpu.roll(x, s, 0), 0.0)
        s *= 2
    return x


def wrap(t, total):
    if total & (total - 1) == 0:
        return t & (total - 1)
    return lax.rem(t, total)


def first_tile(off_ref, planes, p):
    return off_ref[lax.axis_index("depth") * planes + p]


def tile_at(base, j, rays):
    return pl.ds(pl.multiple_of(wrap(base + j, rays // TILE) * TILE, TILE), TILE)


def gather_tiles(off_ref, vox_ref, x_ref, step):
    planes, feats, rays = vox_ref.shape
    tiles = x_ref.shape[1] // TILE
    for p in range(planes):
        base = step * tiles + first_tile(off_ref, planes, p)
        for j in range(tiles):
            x_ref[pl.ds(p * feats, feats), pl.ds(j * TILE, TILE)] = vox_ref[
                p, :, tile_at(base, j, rays)
            ]


def absorb(dens):
    upto = running_sum(dens)
    passing = jnp.exp(-dens)
    before = jnp.exp(dens - upto)
    return upto, passing, before


def softplus(x):
    return jnp.maximum(x, 0.0) + jnp.log1p(jnp.exp(-jnp.abs(x)))


def picks(shape, period, dim):
    other = lax.broadcasted_iota(jnp.int32, shape, 1 - dim)
    return (lax.rem(lax.broadcasted_iota(jnp.int32, shape, dim), period) == other).astype(BF)


def diagonal(shape, rows, cols):
    r = lax.broadcasted_iota(jnp.int32, shape, 0) // rows
    return r == lax.broadcasted_iota(jnp.int32, shape, 1) // cols


def repeat_blocks(w):
    rows, cols = w.shape
    tall = dot(picks((PACK * rows, rows), rows, 0), w).astype(BF)
    full = dot(tall, picks((cols, PACK * cols), cols, 1))
    return jnp.where(diagonal(full.shape, rows, cols), full, 0.0)


def prepare(first_ref, second_ref, w1_ref, w1t_ref, w2_ref, w2t_ref):
    planes = PACK * w2_ref.shape[0]
    chans, hid = second_ref.shape[0] - 1, second_ref.shape[1]
    w1 = repeat_blocks(first_ref[...])
    w1_ref[...] = (0.5 * w1).astype(BF)
    w1t_ref[...] = w1.T.astype(BF)
    rad = repeat_blocks(second_ref[0:chans, :])
    dens = dot(second_ref[chans : chans + 1, :], picks((hid, PACK * hid), hid, 1))
    dens = jnp.broadcast_to(dens, (planes, PACK * hid))
    block = lax.broadcasted_iota(jnp.int32, dens.shape, 1) // hid
    plane = lax.broadcasted_iota(jnp.int32, dens.shape, 0)
    for h in range(planes // PACK):
        mine = jnp.where(plane == block + h * PACK, dens, 0.0)
        w2_ref[h] = jnp.concatenate([0.5 * rad, mine], 0).astype(BF)
        w2t_ref[h] = (0.5 * jnp.concatenate([rad, mine], 0)).T.astype(BF)


def forward_kernel(
    dscale,
    sub,
    off_ref,
    vox_ref,
    first_ref,
    second_ref,
    col_ref,
    last_ref,
    w1_ref,
    w1t_ref,
    w2_ref,
    w2t_ref,
    x_ref,
    rad_ref,
):
    step = pl.program_id(0)

    @pl.when(step == 0)
    def _():
        prepare(first_ref, second_ref, w1_ref, w1t_ref, w2_ref, w2t_ref)

    gather_tiles(off_ref, vox_ref, x_ref, step)
    halves, rows = w2_ref.shape[0], w2_ref.shape[1]
    planes = vox_ref.shape[0]
    wide = rows - planes
    kin = w1_ref.shape[1]
    chans = col_ref.shape[1]
    for c in range(x_ref.shape[1] // sub):
        here = pl.ds(c * sub, sub)
        raw_d = None
        for h in range(halves):
            half = dot(w1_ref[...], x_ref[pl.ds(h * kin, kin), here])
            hidden = (half + half * jnp.tanh(half)).astype(BF)
            raw = dot(w2_ref[h], hidden)
            rad_ref[pl.ds(h * wide, wide), here] = jnp.tanh(raw[:wide])
            d = raw[wide:]
            raw_d = d if raw_d is None else raw_d + d
        dens = softplus(raw_d) * dscale
        upto, passing, before = absorb(dens)
        weight = 0.5 * before * (1.0 - passing)
        colour = jnp.sum(weight, axis=0, keepdims=True)
        for p in range(planes):
            colour = colour + weight[p : p + 1] * rad_ref[pl.ds(p * chans, chans), here]
        col_ref[0, :, here] = colour
        last_ref[0, :, here] = jnp.exp(-upto[planes - 1 : planes])


def backward_kernel(
    dscale,
    sub,
    off_ref,
    vox_ref,
    w1_ref,
    w1t_ref,
    w2_ref,
    w2t_ref,
    cot_ref,
    state_ref,
    gvox_ref,
    acc1_ref,
    acc2_ref,
    x_ref,
    slope_ref,
    hid_ref,
    s_ref,
    graw_ref,
    gpre_ref,
):
    step = pl.program_id(0)

    @pl.when(step == 0)
    def _():
        acc1_ref[...] = jnp.zeros_like(acc1_ref)
        acc2_ref[...] = jnp.zeros_like(acc2_ref)

    gather_tiles(off_ref, vox_ref, x_ref, step)
    halves, rows = w2_ref.shape[0], w2_ref.shape[1]
    planes, feats, rays = vox_ref.shape
    wide = rows - planes
    kin = w1_ref.shape[1]
    kmid = w1_ref.shape[0]
    chans = cot_ref.shape[1]
    width = x_ref.shape[1]
    ones = diagonal((planes, planes * chans), 1, chans).astype(BF)
    for c in range(width // sub):
        here = pl.ds(c * sub, sub)
        cot = cot_ref[0, :, here].astype(F32)
        raw_d = None
        score = 0.5 * jnp.sum(cot, axis=0, keepdims=True)
        for h in range(halves):
            half = dot(w1_ref[...], x_ref[pl.ds(h * kin, kin), here])
            t = jnp.tanh(half)
            up = 1.0 + t
            hidden = half * up
            slope_ref[pl.ds(h * kmid, kmid), here] = up + hidden * (1.0 - t)
            hidden = hidden.astype(BF)
            hid_ref[pl.ds(h * kmid, kmid), here] = hidden
            raw = dot(w2_ref[h], hidden)
            s = jnp.tanh(raw[:wide])
            s_ref[pl.ds(h * wide, wide), here] = s
            prod = jnp.concatenate(
                [(cot * s[k * chans : (k + 1) * chans]).astype(BF) for k in range(PACK)], 0
            )
            score = score + 0.5 * dot(ones[:, h * wide : (h + 1) * wide], prod)
            d = raw[wide:]
            raw_d = d if raw_d is None else raw_d + d
        dens = softplus(raw_d) * dscale
        upto, passing, before = absorb(dens)
        enter = state_ref[0, 0:1, here]
        rest = state_ref[0, 1:2, here]
        before = enter * before
        weight = before * (1.0 - passing)
        running = running_sum(weight * score)
        grad_d = before * passing * score - (rest - running)
        grad_d = (grad_d * (dscale * (0.5 * jnp.tanh(0.5 * raw_d) + 0.5))).astype(BF)
        weight = 0.25 * weight
        for h in range(halves):
            for k in range(PACK):
                p = h * PACK + k
                s = s_ref[pl.ds(p * chans, chans), here]
                graw_ref[h, pl.ds(k * chans, chans), here] = (
                    (weight[p : p + 1] * cot) * (1.0 - s * s)
                ).astype(BF)
            graw_ref[h, pl.ds(wide, planes), here] = grad_d
            ghid = dot(w2t_ref[h], graw_ref[h, :, here])
            gpre = (ghid * slope_ref[pl.ds(h * kmid, kmid), here]).astype(BF)
            gpre_ref[pl.ds(h * kmid, kmid), here] = gpre
            gx = dot(w1t_ref[...], gpre).astype(BF)
            for k in range(PACK):
                p = h * PACK + k
                base = (step * width + c * sub) // TILE + first_tile(off_ref, planes, p)
                for j in range(sub // TILE):
                    gvox_ref[p, :, tile_at(base, j, rays)] = gx[
                        k * feats : (k + 1) * feats, j * TILE : (j + 1) * TILE
                    ]
    for h in range(halves):
        gpre = gpre_ref[pl.ds(h * kmid, kmid), :]
        x = x_ref[pl.ds(h * kin, kin), :]
        hidden = hid_ref[pl.ds(h * kmid, kmid), :]
        acc1_ref[...] += lax.dot_general(gpre, x, NT, preferred_element_type=F32)
        acc2_ref[h] += lax.dot_general(graw_ref[h], hidden, NT, preferred_element_type=F32)


def greet(n, me):
    barrier = pltpu.get_barrier_semaphore()
    for s in range(1, n):
        pl.semaphore_signal(
            barrier,
            inc=1,
            device_id={"depth": lax.rem(me + s, n)},
            device_id_type=pl.DeviceIdType.MESH,
        )
    pl.semaphore_wait(barrier, n - 1)


def swap(n, me, source, target, send_sem, recv_sem):
    copies = []
    for s in range(1, n):
        to = lax.rem(me + s, n)
        copies.append(
            pltpu.make_async_remote_copy(
                src_ref=source(to),
                dst_ref=target.at[me],
                send_sem=send_sem.at[s],
                recv_sem=recv_sem.at[s],
                device_id={"depth": to},
                device_id_type=pl.DeviceIdType.MESH,
            )
        )
    for copy in copies:
        copy.start()
    return copies


def state_kernel(n, last_ref, col_ref, cot_ref, out_ref, mine, got, back, s1, r1, s2, r2):
    me = lax.axis_index("depth")
    greet(n, me)

    def fill(d, carry):
        mine[d, 0:1, :] = last_ref[d]
        mine[d, 1:2, :] = jnp.sum(col_ref[d] * cot_ref[d].astype(F32), axis=0, keepdims=True)
        return carry

    lax.fori_loop(0, n, fill, 0)
    copies = swap(n, me, lambda to: mine.at[to], got, s1, r1)
    got[me] = mine[me]
    for copy in copies:
        copy.wait()
    enter = jnp.ones_like(got[0, 0:1, :])
    prior = jnp.zeros_like(enter)
    for d in range(n):
        back[d, 0:1, :] = enter
        back[d, 1:2, :] = prior
        prior = prior + enter * got[d, 1:2, :]
        enter = enter * got[d, 0:1, :]
    for d in range(n):
        back[d, 1:2, :] = prior - back[d, 1:2, :]
    copies = swap(n, me, lambda to: back.at[to], out_ref, s2, r2)
    out_ref[me] = back[me]
    for copy in copies:
        copy.wait()


def exchange_state(n, last, colour, cot):
    chunk = last.shape[2]
    shape = (n, 2, chunk)
    vmem = pl.BlockSpec(memory_space=pltpu.VMEM)
    return pl.pallas_call(
        functools.partial(state_kernel, n),
        out_shape=jax.ShapeDtypeStruct(shape, F32),
        in_specs=[vmem] * 3,
        out_specs=vmem,
        scratch_shapes=[pltpu.VMEM(shape, F32)] * 3 + [pltpu.SemaphoreType.DMA((n,))] * 4,
        compiler_params=pltpu.CompilerParams(collective_id=1, has_side_effects=True),
        name="exchange_state",
    )(last, colour, cot)


def total_kernel(n, a1_ref, a2_ref, g1_ref, g2_ref, give, got, mine, full, s1, r1, s2, r2):
    me = lax.axis_index("depth")
    greet(n, me)
    hid, feats = g1_ref.shape
    chans = g2_ref.shape[0] - 1
    halves, rows = a2_ref.shape[0], a2_ref.shape[1]
    part = give.shape[1]

    def aligned(ref_rows, k, size):
        at = k * size
        lane = at % TILE
        piece = ref_rows[:, at - lane : at - lane + TILE]
        return pltpu.roll(piece, TILE - lane, 1) if lane else piece

    g1 = g2 = gd = None
    for k in range(PACK):
        one = aligned(a1_ref[pl.ds(k * hid, hid), :], k, feats)
        g1 = one if g1 is None else g1 + one
    for h in range(halves):
        tail = a2_ref[h, pl.ds(PACK * chans, rows - PACK * chans), :]
        row = lax.broadcasted_iota(jnp.int32, (tail.shape[0], TILE), 0)
        for k in range(PACK):
            two = aligned(a2_ref[h, pl.ds(k * chans, chans), :], k, hid)
            g2 = two if g2 is None else g2 + two
            dens = jnp.where(row == h * PACK + k, aligned(tail, k, hid), 0.0)
            dens = jnp.sum(dens, axis=0, keepdims=True)
            gd = dens if gd is None else gd + dens
    lanes = lax.broadcasted_iota(jnp.int32, (hid, TILE), 1)
    rest = hid - chans - 1
    low = jnp.concatenate([g2, gd, jnp.zeros((rest, TILE), F32)], 0)
    both = jnp.where(lanes < hid, low, pltpu.roll(g1, hid, 1))
    for d in range(n):
        give[d] = both[d * part : (d + 1) * part]
    copies = swap(n, me, lambda to: give.at[to], got, s1, r1)
    got[me] = give[me]
    for copy in copies:
        copy.wait()
    mine[...] = jnp.sum(got[...], axis=0)
    copies = swap(n, me, lambda to: mine, full, s2, r2)
    full[me] = mine[...]
    for copy in copies:
        copy.wait()
    both = jnp.concatenate([full[d] for d in range(n)], 0)
    g2_ref[...] = both[: chans + 1, :hid]
    g1_ref[...] = pltpu.roll(both, TILE - hid, 1)[:, :feats]


def total_over_depth(n, acc1, acc2, first, second):
    vmem = pl.BlockSpec(memory_space=pltpu.VMEM)
    part = (n, first[0] // n, TILE)
    return pl.pallas_call(
        functools.partial(total_kernel, n),
        out_shape=(jax.ShapeDtypeStruct(first, F32), jax.ShapeDtypeStruct(second, F32)),
        in_specs=[vmem] * 2,
        out_specs=(vmem, vmem),
        scratch_shapes=[
            pltpu.VMEM(part, F32),
            pltpu.VMEM(part, F32),
            pltpu.VMEM(part[1:], F32),
            pltpu.VMEM(part, F32),
        ]
        + [pltpu.SemaphoreType.DMA((n,))] * 4,
        compiler_params=pltpu.CompilerParams(collective_id=2, has_side_effects=True),
        name="total_over_depth",
    )(acc1, acc2)


def shards(voxels, offsets, w_first, w_second, cotangent):
    planes, feats, rays = voxels.shape
    hid = w_first.shape[0]
    chans, chunk = cotangent.shape
    n = lax.axis_size("depth")
    halves = planes // PACK
    dscale = 3.0 / (planes * n)
    block = min(BLOCK, chunk)
    per = chunk // block
    steps = rays // block
    cot = lax.all_gather(cotangent.astype(BF), "depth")

    smem = pl.BlockSpec(memory_space=pltpu.SMEM)
    vmem = pl.BlockSpec(memory_space=pltpu.VMEM)

    def ray_spec(rows):
        return pl.BlockSpec((1, rows, block), lambda i: (i // per, 0, i % per))

    params = pltpu.CompilerParams(vmem_limit_bytes=60 * 2**20)
    rows = PACK * chans + planes
    weights = (
        jax.ShapeDtypeStruct((PACK * hid, PACK * feats), BF),
        jax.ShapeDtypeStruct((PACK * feats, PACK * hid), BF),
        jax.ShapeDtypeStruct((halves, rows, PACK * hid), BF),
        jax.ShapeDtypeStruct((halves, PACK * hid, rows), BF),
    )
    colour, last, *weights = pl.pallas_call(
        functools.partial(forward_kernel, dscale, min(FSUB, block)),
        grid=(steps,),
        out_shape=(
            jax.ShapeDtypeStruct((n, chans, chunk), F32),
            jax.ShapeDtypeStruct((n, 1, chunk), F32),
        )
        + weights,
        in_specs=[smem] + [vmem] * 3,
        out_specs=(ray_spec(chans), ray_spec(1)) + (vmem,) * 4,
        scratch_shapes=[
            pltpu.VMEM((planes * feats, block), BF),
            pltpu.VMEM((planes * chans, block), F32),
        ],
        compiler_params=params,
        cost_estimate=pl.CostEstimate(
            flops=8 * 10**9, bytes_accessed=12 * 2**20, transcendentals=10**7
        ),
        name="forward",
    )(offsets, voxels, w_first, w_second)
    state = exchange_state(n, last, colour, cot)
    share = (state[:, 0:1, :] * colour).astype(BF)
    image = lax.psum_scatter(share, "depth", scatter_dimension=0).astype(F32)
    gvox, acc1, acc2 = pl.pallas_call(
        functools.partial(backward_kernel, dscale, min(BSUB, block)),
        grid=(steps,),
        out_shape=(
            jax.ShapeDtypeStruct(voxels.shape, BF),
            jax.ShapeDtypeStruct((PACK * hid, PACK * feats), F32),
            jax.ShapeDtypeStruct((halves, rows, PACK * hid), F32),
        ),
        in_specs=[smem] + [vmem] * 5 + [ray_spec(chans), ray_spec(2)],
        out_specs=(vmem, vmem, vmem),
        scratch_shapes=[
            pltpu.VMEM((planes * feats, block), BF),
            pltpu.VMEM((planes * hid, block), F32),
            pltpu.VMEM((planes * hid, block), BF),
            pltpu.VMEM((planes * chans, block), F32),
            pltpu.VMEM((halves, rows, block), BF),
            pltpu.VMEM((planes * hid, block), BF),
        ],
        compiler_params=params,
        cost_estimate=pl.CostEstimate(
            flops=60 * 10**9, bytes_accessed=24 * 2**20, transcendentals=10**7
        ),
        name="backward",
    )(offsets, voxels, *weights, cot, state)
    grad_first, grad_second = total_over_depth(n, acc1, acc2, w_first.shape, w_second.shape)
    return image, gvox, grad_first, grad_second


def solution(mesh):
    placed = (
        P(("groups", "depth"), None, None),
        P("groups"),
        P(),
        P(),
        P(None, ("groups", "depth")),
    )
    return jax.shard_map(
        shards,
        mesh=mesh,
        in_specs=placed,
        out_specs=(
            P(None, ("groups", "depth")),
            P(("groups", "depth"), None, None),
            P("groups", None),
            P("groups", None),
        ),
        check_vma=False,
    )
```

```python
import functools

import jax
import jax.numpy as jnp
from jax import lax
from jax.experimental import pallas as pl
from jax.experimental.pallas import tpu as pltpu
from jax.sharding import PartitionSpec as P

TILE = 128
PACK = 4
BLOCK = 1024
FSUB = 1024
BSUB = 1024
RELAY = 12
BF = jnp.bfloat16
F32 = jnp.float32
NT = (((1,), (1,)), ((), ()))


def dot(a, b):
    return jnp.dot(a, b, preferred_element_type=F32)


def running_sum(x):
    rows = x.shape[0]
    row = lax.broadcasted_iota(jnp.int32, x.shape, 0)
    s = 1
    while s < rows:
        x = x + jnp.where(row >= s, pltpu.roll(x, s, 0), 0.0)
        s *= 2
    return x


def wrap(t, total):
    if total & (total - 1) == 0:
        return t & (total - 1)
    return lax.rem(t, total)


def first_tile(off_ref, planes, p):
    return off_ref[lax.axis_index("depth") * planes + p]


def tile_at(base, j, rays):
    return pl.ds(pl.multiple_of(wrap(base + j, rays // TILE) * TILE, TILE), TILE)


def shear_kernel(off_ref, vox_ref, x_ref):
    rays = vox_ref.shape[2]
    base = first_tile(off_ref, pl.num_programs(0), pl.program_id(0))
    for j in range(rays // TILE):
        x_ref[:, pl.ds(j * TILE, TILE)] = vox_ref[0, :, tile_at(base, j, rays)]


def shear(offsets, voxels):
    planes, feats, rays = voxels.shape
    return pl.pallas_call(
        shear_kernel,
        grid=(planes,),
        out_shape=jax.ShapeDtypeStruct((planes * feats, rays), BF),
        in_specs=[
            pl.BlockSpec(memory_space=pltpu.SMEM),
            pl.BlockSpec((1, feats, rays), lambda p: (p, 0, 0)),
        ],
        out_specs=pl.BlockSpec((feats, rays), lambda p: (p, 0)),
        name="shear",
    )(offsets, voxels)


def absorb(dens):
    upto = running_sum(dens)
    passing = jnp.exp(-dens)
    before = jnp.exp(dens - upto)
    return upto, passing, before


def softplus(x):
    return jnp.maximum(x, 0.0) + jnp.log1p(jnp.exp(-jnp.abs(x)))


def picks(shape, period, dim):
    other = lax.broadcasted_iota(jnp.int32, shape, 1 - dim)
    return (lax.rem(lax.broadcasted_iota(jnp.int32, shape, dim), period) == other).astype(BF)


def diagonal(shape, rows, cols):
    r = lax.broadcasted_iota(jnp.int32, shape, 0) // rows
    return r == lax.broadcasted_iota(jnp.int32, shape, 1) // cols


def repeat_blocks(w):
    rows, cols = w.shape
    tall = dot(picks((PACK * rows, rows), rows, 0), w).astype(BF)
    full = dot(tall, picks((cols, PACK * cols), cols, 1))
    return jnp.where(diagonal(full.shape, rows, cols), full, 0.0)


def prepare(first_ref, second_ref, w1_ref, w1t_ref, w2_ref, w2t_ref):
    planes = PACK * w2_ref.shape[0]
    chans, hid = second_ref.shape[0] - 1, second_ref.shape[1]
    w1 = repeat_blocks(first_ref[...])
    w1_ref[...] = (0.5 * w1).astype(BF)
    w1t_ref[...] = w1.T.astype(BF)
    rad = repeat_blocks(second_ref[0:chans, :])
    dens = dot(second_ref[chans : chans + 1, :], picks((hid, PACK * hid), hid, 1))
    dens = jnp.broadcast_to(dens, (planes, PACK * hid))
    block = lax.broadcasted_iota(jnp.int32, dens.shape, 1) // hid
    plane = lax.broadcasted_iota(jnp.int32, dens.shape, 0)
    for h in range(planes // PACK):
        mine = jnp.where(plane == block + h * PACK, dens, 0.0)
        w2_ref[h] = jnp.concatenate([0.5 * rad, mine], 0).astype(BF)
        w2t_ref[h] = (0.5 * jnp.concatenate([rad, mine], 0)).T.astype(BF)


def forward_kernel(
    dscale,
    sub,
    x_ref,
    first_ref,
    second_ref,
    cot_ref,
    col_ref,
    cots_ref,
    state_ref,
    w1_ref,
    w1t_ref,
    w2_ref,
    w2t_ref,
    rad_ref,
    cots,
    mine,
    got,
    back,
    land,
    sa,
    ra,
    sb,
    rb,
    s1,
    r1,
    s2,
    r2,
):
    step = pl.program_id(0)
    steps = pl.num_programs(0)
    n = mine.shape[0]
    me = lax.axis_index("depth")
    chip, core = me // 2, lax.rem(me, 2)

    def across_chips(s):
        return pltpu.make_async_remote_copy(
            src_ref=cots.at[chip, core],
            dst_ref=cots.at[chip, core],
            send_sem=sa.at[s],
            recv_sem=ra.at[s],
            device_id={"depth": lax.rem(me + 2 * s, n)},
            device_id_type=pl.DeviceIdType.MESH,
        )

    def to_partner():
        return pltpu.make_async_remote_copy(
            src_ref=cots.at[:, core],
            dst_ref=cots.at[:, core],
            send_sem=sb,
            recv_sem=rb,
            device_id={"depth": me + 1 - 2 * core},
            device_id_type=pl.DeviceIdType.MESH,
        )

    @pl.when(step == 0)
    def _():
        cots[chip, core] = cot_ref[...].astype(BF)
        greet(n, me)
        for s in range(1, n // 2):
            across_chips(s).start()
        prepare(first_ref, second_ref, w1_ref, w1t_ref, w2_ref, w2t_ref)

    @pl.when(step == RELAY * steps // 16)
    def _():
        for s in range(1, n // 2):
            across_chips(s).wait()
        to_partner().start()

    halves, rows = w2_ref.shape[0], w2_ref.shape[1]
    planes = PACK * halves
    per = col_ref.shape[2] // x_ref.shape[1]
    wide = rows - planes
    kin = w1_ref.shape[1]
    chans = col_ref.shape[1]
    for c in range(x_ref.shape[1] // sub):
        here = pl.ds(c * sub, sub)
        raw_d = None
        for h in range(halves):
            half = dot(w1_ref[...], x_ref[pl.ds(h * kin, kin), here])
            hidden = (half + half * jnp.tanh(half)).astype(BF)
            raw = dot(w2_ref[h], hidden)
            rad_ref[pl.ds(h * wide, wide), here] = jnp.tanh(raw[:wide])
            d = raw[wide:]
            raw_d = d if raw_d is None else raw_d + d
        dens = softplus(raw_d) * dscale
        upto, passing, before = absorb(dens)
        weight = 0.5 * before * (1.0 - passing)
        colour = jnp.sum(weight, axis=0, keepdims=True)
        for p in range(planes):
            colour = colour + weight[p : p + 1] * rad_ref[pl.ds(p * chans, chans), here]
        at = pl.multiple_of(lax.rem(step, per) * x_ref.shape[1] + c * sub, TILE)
        col_ref[step // per, :, pl.ds(at, sub)] = colour
        mine[step // per, 0:1, pl.ds(at, sub)] = jnp.exp(-upto[planes - 1 : planes])

    @pl.when(step == steps - 1)
    def _():
        to_partner().wait()
        share_state(n, me, col_ref, cots, cots_ref, state_ref, mine, got, back, land, s1, r1, s2, r2)


def backward_kernel(
    dscale,
    sub,
    off_ref,
    x_ref,
    w1_ref,
    w1t_ref,
    w2_ref,
    w2t_ref,
    cot_ref,
    state_ref,
    gvox_ref,
    acc1_ref,
    acc2_ref,
    slope_ref,
    hid_ref,
    s_ref,
    graw_ref,
    gpre_ref,
):
    step = pl.program_id(0)

    @pl.when(step == 0)
    def _():
        acc1_ref[...] = jnp.zeros_like(acc1_ref)
        acc2_ref[...] = jnp.zeros_like(acc2_ref)

    halves, rows = w2_ref.shape[0], w2_ref.shape[1]
    planes, feats, rays = gvox_ref.shape
    wide = rows - planes
    kin = w1_ref.shape[1]
    kmid = w1_ref.shape[0]
    chans = cot_ref.shape[1]
    width = x_ref.shape[1]
    ones = diagonal((planes, planes * chans), 1, chans).astype(BF)
    for c in range(width // sub):
        here = pl.ds(c * sub, sub)
        cot = cot_ref[0, :, here].astype(F32)
        raw_d = None
        score = 0.5 * jnp.sum(cot, axis=0, keepdims=True)
        for h in range(halves):
            half = dot(w1_ref[...], x_ref[pl.ds(h * kin, kin), here])
            t = jnp.tanh(half)
            up = 1.0 + t
            hidden = half * up
            slope_ref[pl.ds(h * kmid, kmid), here] = up + hidden * (1.0 - t)
            hidden = hidden.astype(BF)
            hid_ref[pl.ds(h * kmid, kmid), here] = hidden
            raw = dot(w2_ref[h], hidden)
            s = jnp.tanh(raw[:wide])
            s_ref[pl.ds(h * wide, wide), here] = s
            prod = jnp.concatenate(
                [(cot * s[k * chans : (k + 1) * chans]).astype(BF) for k in range(PACK)], 0
            )
            score = score + 0.5 * dot(ones[:, h * wide : (h + 1) * wide], prod)
            d = raw[wide:]
            raw_d = d if raw_d is None else raw_d + d
        dens = softplus(raw_d) * dscale
        upto, passing, before = absorb(dens)
        enter = state_ref[0, 0:1, here]
        rest = state_ref[0, 1:2, here]
        before = enter * before
        weight = before * (1.0 - passing)
        running = running_sum(weight * score)
        grad_d = before * passing * score - (rest - running)
        grad_d = (grad_d * (dscale * (0.5 * jnp.tanh(0.5 * raw_d) + 0.5))).astype(BF)
        weight = 0.25 * weight
        for h in range(halves):
            for k in range(PACK):
                p = h * PACK + k
                s = s_ref[pl.ds(p * chans, chans), here]
                graw_ref[h, pl.ds(k * chans, chans), here] = (
                    (weight[p : p + 1] * cot) * (1.0 - s * s)
                ).astype(BF)
            graw_ref[h, pl.ds(wide, planes), here] = grad_d
            ghid = dot(w2t_ref[h], graw_ref[h, :, here])
            gpre = (ghid * slope_ref[pl.ds(h * kmid, kmid), here]).astype(BF)
            gpre_ref[pl.ds(h * kmid, kmid), here] = gpre
            gx = dot(w1t_ref[...], gpre).astype(BF)
            for k in range(PACK):
                p = h * PACK + k
                base = (step * width + c * sub) // TILE + first_tile(off_ref, planes, p)
                for j in range(sub // TILE):
                    gvox_ref[p, :, tile_at(base, j, rays)] = gx[
                        k * feats : (k + 1) * feats, j * TILE : (j + 1) * TILE
                    ]
    for h in range(halves):
        gpre = gpre_ref[pl.ds(h * kmid, kmid), :]
        x = x_ref[pl.ds(h * kin, kin), :]
        hidden = hid_ref[pl.ds(h * kmid, kmid), :]
        acc1_ref[...] += lax.dot_general(gpre, x, NT, preferred_element_type=F32)
        acc2_ref[h] += lax.dot_general(graw_ref[h], hidden, NT, preferred_element_type=F32)


def greet(n, me):
    barrier = pltpu.get_barrier_semaphore()
    for s in range(1, n):
        pl.semaphore_signal(
            barrier,
            inc=1,
            device_id={"depth": lax.rem(me + s, n)},
            device_id_type=pl.DeviceIdType.MESH,
        )
    pl.semaphore_wait(barrier, n - 1)


def swap(n, me, source, target, send_sem, recv_sem):
    copies = []
    for s in range(1, n):
        to = lax.rem(me + s, n)
        copies.append(
            pltpu.make_async_remote_copy(
                src_ref=source(to),
                dst_ref=target.at[me],
                send_sem=send_sem.at[s],
                recv_sem=recv_sem.at[s],
                device_id={"depth": to},
                device_id_type=pl.DeviceIdType.MESH,
            )
        )
    for copy in copies:
        copy.start()
    return copies


def share_state(n, me, col_ref, cots, cots_ref, state_ref, mine, got, back, land, s1, r1, s2, r2):
    def fill(q, carry):
        for core in range(2):
            cot = cots[q, core]
            cots_ref[q, core] = cot
            d = 2 * q + core
            mine[d, 1:2, :] = jnp.sum(col_ref[d] * cot.astype(F32), axis=0, keepdims=True)
        return carry

    lax.fori_loop(0, n // 2, fill, 0)
    copies = swap(n, me, lambda to: mine.at[to], got, s1, r1)
    got[me] = mine[me]
    for copy in copies:
        copy.wait()
    enter = jnp.ones_like(got[0, 0:1, :])
    prior = jnp.zeros_like(enter)
    for d in range(n):
        back[d, 0:1, :] = enter
        back[d, 1:2, :] = prior
        prior = prior + enter * got[d, 1:2, :]
        enter = enter * got[d, 0:1, :]
    for d in range(n):
        back[d, 1:2, :] = prior - back[d, 1:2, :]
    copies = swap(n, me, lambda to: back.at[to], land, s2, r2)
    land[me] = back[me]
    for copy in copies:
        copy.wait()
    state_ref[...] = land[...]


def total_kernel(n, a1_ref, a2_ref, g1_ref, g2_ref, give, got, mine, full, s1, r1, s2, r2):
    me = lax.axis_index("depth")
    greet(n, me)
    hid, feats = g1_ref.shape
    chans = g2_ref.shape[0] - 1
    halves, rows = a2_ref.shape[0], a2_ref.shape[1]
    part = give.shape[1]

    def aligned(ref_rows, k, size):
        at = k * size
        lane = at % TILE
        piece = ref_rows[:, at - lane : at - lane + TILE]
        return pltpu.roll(piece, TILE - lane, 1) if lane else piece

    g1 = g2 = gd = None
    for k in range(PACK):
        one = aligned(a1_ref[pl.ds(k * hid, hid), :], k, feats)
        g1 = one if g1 is None else g1 + one
    for h in range(halves):
        tail = a2_ref[h, pl.ds(PACK * chans, rows - PACK * chans), :]
        row = lax.broadcasted_iota(jnp.int32, (tail.shape[0], TILE), 0)
        for k in range(PACK):
            two = aligned(a2_ref[h, pl.ds(k * chans, chans), :], k, hid)
            g2 = two if g2 is None else g2 + two
            dens = jnp.where(row == h * PACK + k, aligned(tail, k, hid), 0.0)
            dens = jnp.sum(dens, axis=0, keepdims=True)
            gd = dens if gd is None else gd + dens
    lanes = lax.broadcasted_iota(jnp.int32, (hid, TILE), 1)
    rest = hid - chans - 1
    low = jnp.concatenate([g2, gd, jnp.zeros((rest, TILE), F32)], 0)
    both = jnp.where(lanes < hid, low, pltpu.roll(g1, hid, 1))
    for d in range(n):
        give[d] = both[d * part : (d + 1) * part]
    copies = swap(n, me, lambda to: give.at[to], got, s1, r1)
    got[me] = give[me]
    for copy in copies:
        copy.wait()
    mine[...] = jnp.sum(got[...], axis=0)
    copies = swap(n, me, lambda to: mine, full, s2, r2)
    full[me] = mine[...]
    for copy in copies:
        copy.wait()
    both = jnp.concatenate([full[d] for d in range(n)], 0)
    g2_ref[...] = both[: chans + 1, :hid]
    g1_ref[...] = pltpu.roll(both, TILE - hid, 1)[:, :feats]


def total_over_depth(n, acc1, acc2, first, second):
    vmem = pl.BlockSpec(memory_space=pltpu.VMEM)
    part = (n, first[0] // n, TILE)
    return pl.pallas_call(
        functools.partial(total_kernel, n),
        out_shape=(jax.ShapeDtypeStruct(first, F32), jax.ShapeDtypeStruct(second, F32)),
        in_specs=[vmem] * 2,
        out_specs=(vmem, vmem),
        scratch_shapes=[
            pltpu.VMEM(part, F32),
            pltpu.VMEM(part, F32),
            pltpu.VMEM(part[1:], F32),
            pltpu.VMEM(part, F32),
        ]
        + [pltpu.SemaphoreType.DMA((n,))] * 4,
        compiler_params=pltpu.CompilerParams(collective_id=2, has_side_effects=True),
        name="total_over_depth",
    )(acc1, acc2)


def shards(voxels, offsets, w_first, w_second, cotangent):
    planes, feats, rays = voxels.shape
    hid = w_first.shape[0]
    chans, chunk = cotangent.shape
    n = lax.axis_size("depth")
    halves = planes // PACK
    dscale = 3.0 / (planes * n)
    block = min(BLOCK, chunk)
    per = chunk // block
    steps = rays // block

    smem = pl.BlockSpec(memory_space=pltpu.SMEM)
    vmem = pl.BlockSpec(memory_space=pltpu.VMEM)

    def ray_spec(rows):
        return pl.BlockSpec((1, rows, block), lambda i: (i // per, 0, i % per))

    params = pltpu.CompilerParams(vmem_limit_bytes=60 * 2**20)
    rows = PACK * chans + planes
    weights = (
        jax.ShapeDtypeStruct((PACK * hid, PACK * feats), BF),
        jax.ShapeDtypeStruct((PACK * feats, PACK * hid), BF),
        jax.ShapeDtypeStruct((halves, rows, PACK * hid), BF),
        jax.ShapeDtypeStruct((halves, PACK * hid, rows), BF),
    )
    x_spec = pl.BlockSpec((planes * feats, block), lambda i: (0, i))
    sheared = shear(offsets, voxels)
    halved = (n // 2, 2, chans, chunk)
    pair = (n, 2, chunk)
    colour, cot, state, *weights = pl.pallas_call(
        functools.partial(forward_kernel, dscale, min(FSUB, block)),
        grid=(steps,),
        out_shape=(
            jax.ShapeDtypeStruct((n, chans, chunk), F32),
            jax.ShapeDtypeStruct(halved, BF),
            jax.ShapeDtypeStruct(pair, F32),
        )
        + weights,
        in_specs=[x_spec] + [vmem] * 3,
        out_specs=(vmem,) * 7,
        scratch_shapes=[
            pltpu.VMEM((planes * chans, block), F32),
            pltpu.VMEM(halved, BF),
        ]
        + [pltpu.VMEM(pair, F32)] * 4
        + [pltpu.SemaphoreType.DMA((n // 2,))] * 2
        + [pltpu.SemaphoreType.DMA] * 2
        + [pltpu.SemaphoreType.DMA((n,))] * 4,
        compiler_params=pltpu.CompilerParams(
            vmem_limit_bytes=60 * 2**20, collective_id=1, has_side_effects=True
        ),
        cost_estimate=pl.CostEstimate(
            flops=8 * 10**9, bytes_accessed=12 * 2**20, transcendentals=10**7
        ),
        name="forward",
    )(sheared, w_first, w_second, cotangent)
    cot = cot.reshape(n, chans, chunk)
    share = (state[:, 0:1, :] * colour).astype(BF)
    image = lax.psum_scatter(share, "depth", scatter_dimension=0).astype(F32)
    gvox, acc1, acc2 = pl.pallas_call(
        functools.partial(backward_kernel, dscale, min(BSUB, block)),
        grid=(steps,),
        out_shape=(
            jax.ShapeDtypeStruct(voxels.shape, BF),
            jax.ShapeDtypeStruct((PACK * hid, PACK * feats), F32),
            jax.ShapeDtypeStruct((halves, rows, PACK * hid), F32),
        ),
        in_specs=[smem, x_spec] + [vmem] * 4 + [ray_spec(chans), ray_spec(2)],
        out_specs=(vmem, vmem, vmem),
        scratch_shapes=[
            pltpu.VMEM((planes * hid, block), F32),
            pltpu.VMEM((planes * hid, block), BF),
            pltpu.VMEM((planes * chans, block), F32),
            pltpu.VMEM((halves, rows, block), BF),
            pltpu.VMEM((planes * hid, block), BF),
        ],
        compiler_params=params,
        cost_estimate=pl.CostEstimate(
            flops=60 * 10**9, bytes_accessed=24 * 2**20, transcendentals=10**7
        ),
        name="backward",
    )(offsets, sheared, *weights, cot, state)
    grad_first, grad_second = total_over_depth(n, acc1, acc2, w_first.shape, w_second.shape)
    return image, gvox, grad_first, grad_second


def solution(mesh):
    placed = (
        P(("groups", "depth"), None, None),
        P("groups"),
        P(),
        P(),
        P(None, ("groups", "depth")),
    )
    return jax.shard_map(
        shards,
        mesh=mesh,
        in_specs=placed,
        out_specs=(
            P(None, ("groups", "depth")),
            P(("groups", "depth"), None, None),
            P("groups", None),
            P("groups", None),
        ),
        check_vma=False,
    )
```
